256 devices in a mesh: day: 8 (over z_hi, core), row: 32 (over z_lo, x, y).
Axes of the slice: x: 4, y: 4, z: 8 (z_hi: 4, z_lo: 2; z = z_hi * 2 + z_lo), core: 2. Of those that a mesh axis runs over, the one named last changes fastest.
Arguments:
- field: float32 [128, 1024, 1024], P('day', 'row'), may hold values from -6 to 6
- basis_day: float32 [128, 128], replicated, as said below
- basis_x: float32 [1024, 1024], replicated, as said below
- basis_y: float32 [1024, 1024], replicated, as said below
- eig_day: float32 [128], replicated, may hold values from 0.05 to 3
- eig_x: float32 [1024], replicated, may hold values from 0.05 to 3
- eig_y: float32 [1024], replicated, may hold values from 0.05 to 3
- noise: float32 [1], replicated, may hold values from 0.1 to 0.5
Outputs:
- weights: float32 [128, 1024, 1024], P('day', 'row')
The draws below stay inside these ranges and needn't reach their ends.
Inputs may be any that keep to these rules, and one draw needn't show every extreme that they name: basis_day is orthogonal. basis_x is orthogonal. basis_y is orthogonal.
All inputs are finite; a program needn't handle non-finite values.
Results may differ from the reference program's by a relative error of at most 0.00007.
Values sent between devices are 32-bit elements; how exact they have to be, the bound alone decides.
No kernel may reach another device: no remote copies, remote signals or barrier semaphores. Data moves between devices by JAX's collectives and lax.ppermute only.
A program may use at most 128 MiB of HBM per device.

```python
import math
import jax
import jax.numpy as jnp
from jax import lax

DAYS = 128
NX = 1024
NY = 1024


def orthogonal(key, order):
    matrix = jax.random.normal(key, (order, order), jnp.float32)
    factor, upper = jnp.linalg.qr(matrix)
    return factor


def draw_basis_day(key, part):
    return orthogonal(jax.random.fold_in(key, 11), DAYS)


def draw_basis_x(key, part):
    return orthogonal(jax.random.fold_in(key, 23), NX)


def draw_basis_y(key, part):
    return orthogonal(jax.random.fold_in(key, 37), NY)


def levels(own_key, shape, cuts, low, high):
    def one(position, parts):
        draws = jax.random.uniform(jax.random.fold_in(jax.random.fold_in(own_key, 6), position), (parts,), jnp.float32, low / len(cuts), high / len(cuts))
        return jnp.repeat(jnp.exp(draws), shape[position] // parts).reshape((-1,) + (1,) * (len(shape) - position - 1))

    loudness = one(*cuts[0])
    for cut in cuts[1:]:
        loudness = loudness * one(*cut)
    return loudness


def normal_values(rng, extent, deviation, limit, pieces=(), kind=jnp.bfloat16):
    loudness = levels(rng, extent, pieces, -0.22, 0.18) if pieces else 1.0
    result = jax.random.normal(rng, extent, jnp.float32) * deviation * loudness
    return jnp.minimum(jnp.maximum(result, -limit), limit).astype(kind)


def setup_inputs(seed: int = 0) -> dict:
    key_of = jax.random.split(jax.random.key(seed), 9)
    return {
        "field": normal_values(key_of[0], (DAYS, NX, NY), 1.0, 6.0, ((0, 8), (1, 32)), jnp.float32),
        "basis_day": draw_basis_day(jax.random.fold_in(key_of[8], 71), 0),
        "basis_x": draw_basis_x(jax.random.fold_in(key_of[8], 71), 0),
        "basis_y": draw_basis_y(jax.random.fold_in(key_of[8], 71), 0),
        "eig_day": jnp.clip(jnp.exp(jax.random.uniform(key_of[4], (DAYS,), jnp.float32, math.log(0.05), math.log(3.0))), 0.05, 3.0),
        "eig_x": jnp.clip(jnp.exp(jax.random.uniform(key_of[5], (NX,), jnp.float32, math.log(0.05), math.log(3.0))), 0.05, 3.0),
        "eig_y": jnp.clip(jnp.exp(jax.random.uniform(key_of[6], (NY,), jnp.float32, math.log(0.05), math.log(3.0))), 0.05, 3.0),
        "noise": jnp.clip(jnp.exp(jax.random.uniform(key_of[7], (1,), jnp.float32, math.log(0.1), math.log(0.5))), 0.1, 0.5),
    }


def reference(field, basis_day, basis_x, basis_y, eig_day, eig_x, eig_y, noise):
    precise = lax.Precision.HIGHEST
    along_y = jnp.einsum('txy,yb->txb', field, basis_y, precision=precise)
    along_x = jnp.einsum('txb,xa->tab', along_y, basis_x, precision=precise)
    spectral = jnp.einsum('tab,ts->sab', along_x, basis_day, precision=precise)
    spectrum = eig_day[:, None, None] * eig_x[None, :, None] * eig_y[None, None, :] + noise[0]
    scaled = spectral / spectrum
    back_day = jnp.einsum('sab,ts->tab', scaled, basis_day, precision=precise)
    back_x = jnp.einsum('tab,xa->txb', back_day, basis_x, precision=precise)
    return jnp.einsum('txb,yb->txy', back_x, basis_y, precision=precise)
```

```python
import functools

import jax
import jax.numpy as jnp
from jax import lax
from jax.experimental import pallas as pl
from jax.experimental.pallas import tpu as pltpu
from jax.sharding import Mesh, PartitionSpec as P

F32, BF16 = jnp.float32, jnp.bfloat16
AXES = ("zh", "core", "zl", "x", "y")
NB = 2
ROWS = NB * 256


def split(v):
    hi = v.astype(BF16)
    return hi, (v - hi.astype(F32)).astype(BF16)


def dot3(a, b, dims=((1,), (0,))):
    mul = functools.partial(
        lax.dot_general, dimension_numbers=(dims, ((), ())), preferred_element_type=F32
    )
    return mul(a[0], b[0]) + (mul(a[0], b[1]) + mul(a[1], b[0]))


def swap_groups(v):
    group = lax.broadcasted_iota(jnp.int32, v[0].shape, 1) // 32
    low, even = group < 2, group % 2 == 0

    def pair(a, b, keep, left, right):
        return (
            jnp.where(keep, a, pltpu.roll(b, right, 1)),
            jnp.where(keep, pltpu.roll(a, left, 1), b),
        )

    a0, a2 = pair(v[0], v[2], low, 64, 64)
    a1, a3 = pair(v[1], v[3], low, 64, 64)
    w0, w1 = pair(a0, a1, even, 96, 32)
    w2, w3 = pair(a2, a3, even, 96, 32)
    return w0, w1, w2, w3


def forward_y(z_ref, f_ref, by_ref, *refs):
    pieces, (byh_ref, byl_ref, cols) = refs[:8], refs[8:]
    by = split(by_ref[...])
    byh_ref[...], byl_ref[...] = by
    cols[...] = dot3(split(f_ref[...]), by).T
    for k in range(8):
        start = lax.rem(z_ref[0] + k, 8) * 32
        for bl in range(NB):
            rows = pl.ds(pl.multiple_of(bl * 256 + start, 32), 32)
            for q in range(4):
                pieces[k][pl.ds(bl * 4 + q, 32, stride=4 * NB), :] = cols[
                    rows, pl.ds(q * 128, 128)
                ]


def middle(z_ref, noise_ref, r_ref, bxh_ref, bxl_ref, to_ref, back_ref, ed_ref, ey_ref, ex_ref, *refs):
    pieces, (work,) = refs[:8], refs[8:]
    w = 4 * NB

    def place(z, core, tl, x):
        zh, zl = z // 2, lax.rem(z, 2)
        row = pl.multiple_of(((zh * 2 + core) * 4 + tl) * w, w)
        return pl.ds(row, w), pl.ds(pl.multiple_of((zl * 4 + x) * 128, 128), 128)

    for k in range(8):
        z = lax.rem(z_ref[0] - k + 8, 8)
        for core in range(2):
            for x in range(4):
                got = [
                    r_ref[pl.ds(((core * 16 + x * 4 + y) * 8 + k) * w, w), :]
                    for y in range(4)
                ]
                for tl, part in enumerate(swap_groups(got)):
                    work[place(z, core, tl, x)] = part
    bx = bxh_ref[...], bxl_ref[...]
    along_x = dot3(split(work[...]), bx)
    spectral = dot3(split(to_ref[...]), split(along_x))
    spectrum = (ed_ref[...] * ex_ref[...]) * ey_ref[...] + noise_ref[0]
    back_day = dot3(split(back_ref[...]), split(spectral / spectrum))
    work[...] = dot3(split(back_day), bx, ((1,), (1,)))
    for k in range(8):
        z = lax.rem(z_ref[0] + k, 8)
        for core in range(2):
            for x in range(4):
                got = [work[place(z, core, tl, x)] for tl in range(4)]
                for y, part in enumerate(swap_groups(got)):
                    pieces[k][pl.ds((core * 16 + x * 4 + y) * w, w), :] = part


def inverse_y(z_ref, r_ref, byh_ref, byl_ref, *refs):
    before, (out_ref, cols) = refs[:-2], refs[-2:]
    for k in range(8):
        start = lax.rem(z_ref[0] - k + 8, 8) * 32
        for bl in range(NB):
            rows = pl.ds(pl.multiple_of(bl * 256 + start, 32), 32)
            for q in range(4):
                cols[rows, pl.ds(q * 128, 128)] = r_ref[
                    pl.ds(k * 4 * NB + bl * 4 + q, 32, stride=32 * NB), :
                ]
    total = dot3(split(cols[...].T), (byh_ref[...], byl_ref[...]), ((1,), (1,)))
    for ref in before:
        total = total + ref[...]
    out_ref[...] = total


def split_kernel(b_ref, hi_ref, lo_ref):
    hi_ref[...], lo_ref[...] = split(b_ref[...])


VMEM = pl.BlockSpec(memory_space=pltpu.VMEM)
SMEM = pl.BlockSpec(memory_space=pltpu.SMEM)
PIECE = jax.ShapeDtypeStruct((32 * 4 * NB, 128), F32)


def call(kernel, out_shape, n_in, n_smem, scratch=(), mib=40, name=None):
    return pl.pallas_call(
        kernel,
        out_shape=out_shape,
        in_specs=[SMEM] * n_smem + [VMEM] * (n_in - n_smem),
        out_specs=jax.tree.map(lambda _: VMEM, out_shape),
        scratch_shapes=scratch,
        compiler_params=pltpu.CompilerParams(vmem_limit_bytes=mib << 20),
        name=name,
    )


def z_pairs(k):
    pairs = []
    for zh in range(4):
        for zl in range(2):
            z = (zh * 2 + zl + k) % 8
            pairs += [
                (
                    ((zh * 2 + core) * 2 + zl) * 16 + xy,
                    ((z // 2 * 2 + core) * 2 + z % 2) * 16 + xy,
                )
                for core in range(2)
                for xy in range(16)
            ]
    return pairs


def exchange(pieces):
    w = 4 * NB
    order = (1, 7, 2, 6, 3, 5, 4)
    got = {0: pieces[0]}
    for k in order:
        got[k] = lax.ppermute(pieces[k], AXES, z_pairs(k))
    packed = jnp.stack([got[k].reshape(32, w, 128) for k in range(8)], 1)
    packed = lax.all_to_all(packed, ("core", "x", "y"), 0, 0, tiled=True)
    return packed.reshape(32 * 8 * w, 128)


def body(field, basis_day, basis_x, basis_y, eig_day, eig_x, eig_y, noise):
    days, rows, cols = field.shape
    chunks = cols // ROWS
    z = lax.axis_index("zh") * 2 + lax.axis_index("zl")
    mine = z * 32 + lax.axis_index(("core", "x", "y"))
    z = z.astype(jnp.int32).reshape(1)
    flat = field.reshape(days * rows, cols)

    def by_group(v):
        return v.reshape(8, 4, 4, -1).transpose(0, 2, 1, 3).reshape(128, -1)

    ordered = by_group(by_group(basis_day).T)
    to_s = ordered.reshape(32, 1, 4, 32, 1, 4) * jnp.eye(NB, dtype=F32).reshape(1, NB, 1, 1, NB, 1)
    to_s = to_s.reshape(128 * NB, 128 * NB)
    to_t = to_s.T
    ed = jnp.broadcast_to(by_group(eig_day).reshape(32, 1, 4), (32, NB, 4)).reshape(-1, 1)
    ey_mine = lax.dynamic_slice_in_dim(eig_y.reshape(chunks * NB, 256), mine, 1, 1)
    ex = eig_x.reshape(1, -1)
    half = jax.ShapeDtypeStruct((cols, ROWS), BF16)
    square = jax.ShapeDtypeStruct(basis_x.shape, BF16)

    sent, bases = [], []
    for c in range(chunks):
        *pieces, byh, byl = call(
            forward_y, [PIECE] * 8 + [half] * 2, 3, 1, [pltpu.VMEM((ROWS, days * rows), F32)], name="forward_y"
        )(z, flat, basis_y[:, c * ROWS : (c + 1) * ROWS])
        sent.append(pieces)
        bases.append((byh, byl))
    bxh, bxl = call(split_kernel, [square] * 2, 1, 0, name="split_x")(basis_x)
    solved = []
    for c in range(chunks):
        ey = jnp.broadcast_to(ey_mine[c * NB : (c + 1) * NB].reshape(1, NB, 1), (32, NB, 4)).reshape(-1, 1)
        pieces = call(
            middle, [PIECE] * 8, 10, 2, [pltpu.VMEM((128 * NB, cols), F32)], name="middle"
        )(z, noise, exchange(sent[c]), bxh, bxl, to_s, to_t, ed, ey, ex)
        solved.append(pieces)
    total = ()
    for c in range(chunks):
        total = (
            call(
                inverse_y,
                jax.ShapeDtypeStruct(flat.shape, F32),
                4 + len(total),
                1,
                [pltpu.VMEM((ROWS, days * rows), F32)],
                name="inverse_y",
            )(z, exchange(solved[c]), *bases[c], *total),
        )
    return total[0].reshape(days, rows, cols)


def solution(mesh):
    fine = Mesh(mesh.devices.reshape(4, 2, 2, 4, 4), AXES)
    spec = P(("zh", "core"), ("zl", "x", "y"), None)
    in_specs = (spec, P(), P(), P(), P(), P(), P(), P())
    return jax.shard_map(body, mesh=fine, in_specs=in_specs, out_specs=spec, check_vma=False)
```

```python
import functools
import itertools

import jax
import jax.numpy as jnp
from jax import lax
from jax.experimental import pallas as pl
from jax.experimental.pallas import tpu as pltpu
from jax.sharding import Mesh, PartitionSpec as P

F32, BF16 = jnp.float32, jnp.bfloat16
AXES = ("zh", "core", "zl", "x", "y")
ORDER = ("zh", "zl", "core", "x", "y")
NB = 2
ROWS = NB * 256
WIDE = 16


def split(v):
    hi = v.astype(BF16)
    return hi, (v - hi.astype(F32)).astype(BF16)


def dot3(a, b, dims=((1,), (0,))):
    mul = functools.partial(
        lax.dot_general, dimension_numbers=(dims, ((), ())), preferred_element_type=F32
    )
    return mul(a[0], b[0]) + (mul(a[0], b[1]) + mul(a[1], b[0]))


def swap_groups(v):
    group = lax.broadcasted_iota(jnp.int32, v[0].shape, 1) // 32
    low, even = group < 2, group % 2 == 0

    def pair(a, b, keep, left, right):
        return (
            jnp.where(keep, a, pltpu.roll(b, right, 1)),
            jnp.where(keep, pltpu.roll(a, left, 1), b),
        )

    a0, a2 = pair(v[0], v[2], low, 64, 64)
    a1, a3 = pair(v[1], v[3], low, 64, 64)
    w0, w1 = pair(a0, a1, even, 96, 32)
    w2, w3 = pair(a2, a3, even, 96, 32)
    return w0, w1, w2, w3


def forward_y(f_ref, by_ref, out_ref, cols):
    half = pl.program_id(0)
    cols[...] = dot3(split(f_ref[...]), split(by_ref[...])).T
    for bl in range(NB):
        for q in range(4):
            row = half * (4 * NB) + (bl * 4 + q)
            out_ref[pl.ds(row, 256, stride=WIDE), :] = cols[
                pl.ds(bl * 256, 256), pl.ds(q * 128, 128)
            ]


def row_index(shape, dim):
    m = lax.broadcasted_iota(jnp.int32, shape, dim)
    bl = m // 4 % NB
    group, tl, q = m // (16 * NB), m // (4 * NB) % 4, m % 4
    return group * 16 + q * 4 + tl, bl


def day_matrices(basis_day):
    n = 128 * NB
    wide = row_index((n, 128), 0)[0] == lax.broadcasted_iota(jnp.int32, (n, 128), 1)
    tall = row_index((128, n), 1)[0] == lax.broadcasted_iota(jnp.int32, (128, n), 0)
    same = row_index((n, n), 0)[1] == row_index((n, n), 1)[1]
    wide, tall = wide.astype(BF16), tall.astype(BF16)

    def pick(half, dim):
        rows = lax.dot_general(wide, half, (((1,), (dim,)), ((), ())), preferred_element_type=F32)
        both = jnp.dot(rows.astype(BF16), tall, preferred_element_type=F32)
        return jnp.where(same, both, 0.0).astype(BF16)

    halves = split(basis_day)
    return [pick(h, 1) for h in halves], [pick(h, 0) for h in halves]


def middle(mine_ref, noise_ref, eig_y_ref, r_ref, bx_ref, bd_ref, ed_ref, ex_ref, out_ref, work):
    bx = split(bx_ref[...])
    to_s, to_t = day_matrices(bd_ref[...])
    day, bl = row_index((128 * NB, 128), 0)
    chosen = day == lax.broadcasted_iota(jnp.int32, day.shape, 1)
    ed = jnp.sum(jnp.where(chosen, ed_ref[...], 0.0), 1, keepdims=True)
    edx = ed * ex_ref[...]
    w = 4 * NB

    def blocks(half):
        for zh, zl, core, x in itertools.product(range(4), range(2), range(2), range(4)):
            device = ((zh * 2 + zl) * 2 + core) * 16 + x * 4
            ys = [pl.ds((device + y) * WIDE + half * w, w) for y in range(4)]
            tls = [pl.ds(((zh * 2 + core) * 4 + tl) * w, w) for tl in range(4)]
            yield ys, tls, pl.ds((zl * 4 + x) * 128, 128)

    for half in range(WIDE // w):
        first = half * ROWS
        for ys, tls, lanes in blocks(half):
            for rows, part in zip(tls, swap_groups([r_ref[y, :] for y in ys])):
                work[rows, lanes] = part
        ey = jnp.full(ed.shape, eig_y_ref[first + mine_ref[0]], F32)
        for i in range(1, NB):
            ey = jnp.where(bl[:, :1] == i, eig_y_ref[first + i * 256 + mine_ref[0]], ey)
        along_x = dot3(split(work[...]), bx)
        spectral = dot3(to_s, split(along_x))
        back_day = dot3(to_t, split(spectral / (edx * ey + noise_ref[0])))
        work[...] = dot3(split(back_day), bx, ((1,), (1,)))
        for ys, tls, lanes in blocks(half):
            for rows, part in zip(ys, swap_groups([work[t, lanes] for t in tls])):
                out_ref[rows, :] = part


def inverse_y(r_ref, by_ref, out_ref, cols):
    for bl in range(WIDE // 4):
        for q in range(4):
            cols[pl.ds(bl * 256, 256), pl.ds(q * 128, 128)] = r_ref[
                pl.ds(bl * 4 + q, 256, stride=WIDE), :
            ]
    out_ref[...] = dot3(split(cols[...].T), split(by_ref[...]), ((1,), (1,)))


VMEM = pl.BlockSpec(memory_space=pltpu.VMEM)
SMEM = pl.BlockSpec(memory_space=pltpu.SMEM)
PARAMS = pltpu.CompilerParams(vmem_limit_bytes=40 << 20)


def exchange(flat):
    parts = flat.reshape(256, WIDE, 128)
    return lax.all_to_all(parts, ORDER, 0, 0, tiled=True).reshape(flat.shape)


def body(field, basis_day, basis_x, basis_y, eig_day, eig_x, eig_y, noise):
    days, rows, cols = field.shape
    mine = lax.axis_index(ORDER).astype(jnp.int32).reshape(1)
    flat = field.reshape(days * rows, cols)
    wire = jax.ShapeDtypeStruct((256 * WIDE, 128), F32)
    sent = pl.pallas_call(
        forward_y,
        out_shape=wire,
        grid=(cols // ROWS,),
        in_specs=[
            pl.BlockSpec(flat.shape, lambda c: (0, 0)),
            pl.BlockSpec((cols, ROWS), lambda c: (0, c)),
        ],
        out_specs=pl.BlockSpec(wire.shape, lambda c: (0, 0)),
        scratch_shapes=[pltpu.VMEM((ROWS, days * rows), F32)],
        compiler_params=PARAMS,
        name="forward_y",
    )(flat, basis_y)
    solved = pl.pallas_call(
        middle,
        out_shape=wire,
        in_specs=[SMEM] * 3 + [VMEM] * 5,
        out_specs=VMEM,
        scratch_shapes=[pltpu.VMEM((128 * NB, cols), F32)],
        compiler_params=PARAMS,
        name="middle",
    )(mine, noise, eig_y, exchange(sent), basis_x, basis_day, eig_day.reshape(1, -1), eig_x.reshape(1, -1))
    weights = pl.pallas_call(
        inverse_y,
        out_shape=jax.ShapeDtypeStruct(flat.shape, F32),
        in_specs=[VMEM] * 2,
        out_specs=VMEM,
        scratch_shapes=[pltpu.VMEM((cols, days * rows), F32)],
        compiler_params=PARAMS,
        name="inverse_y",
    )(exchange(solved), basis_y)
    return weights.reshape(days, rows, cols)


def solution(mesh):
    fine = Mesh(mesh.devices.reshape(4, 2, 2, 4, 4), AXES)
    spec = P(("zh", "core"), ("zl", "x", "y"), None)
    in_specs = (spec, P(), P(), P(), P(), P(), P(), P())
    return jax.shard_map(body, mesh=fine, in_specs=in_specs, out_specs=spec, check_vma=False)
```

```python
import functools
import itertools

import jax
import jax.numpy as jnp
from jax import lax
from jax.experimental import pallas as pl
from jax.experimental.pallas import tpu as pltpu
from jax.sharding import Mesh, PartitionSpec as P

F32, BF16 = jnp.float32, jnp.bfloat16
AXES = ("zh", "core", "zl", "x", "y")
ORDER = ("zh", "zl", "core", "x", "y")
NB = 2
ROWS = NB * 256
WIDE = 16


def split(v):
    hi = v.astype(BF16)
    return hi, (v - hi.astype(F32)).astype(BF16)


def dot3(a, b, dims=((1,), (0,))):
    mul = functools.partial(
        lax.dot_general, dimension_numbers=(dims, ((), ())), preferred_element_type=F32
    )
    return mul(a[0], b[0]) + (mul(a[0], b[1]) + mul(a[1], b[0]))


def swap_groups(v):
    group = lax.broadcasted_iota(jnp.int32, v[0].shape, 1) // 32
    low, even = group < 2, group % 2 == 0

    def pair(a, b, keep, left, right):
        return (
            jnp.where(keep, a, pltpu.roll(b, right, 1)),
            jnp.where(keep, pltpu.roll(a, left, 1), b),
        )

    a0, a2 = pair(v[0], v[2], low, 64, 64)
    a1, a3 = pair(v[1], v[3], low, 64, 64)
    w0, w1 = pair(a0, a1, even, 96, 32)
    w2, w3 = pair(a2, a3, even, 96, 32)
    return w0, w1, w2, w3


def forward_y(noise_ref, f_ref, by_ref, out_ref, level_ref, cols):
    level_ref[...] = jnp.full(level_ref.shape, noise_ref[0], F32)
    cols[...] = dot3(split(by_ref[...]), split(f_ref[...]), ((0,), (1,)))
    out = out_ref.reshape(256 * 4 * NB, 128)
    for bl in range(NB):
        for q in range(4):
            out[pl.ds(bl * 4 + q, 256, stride=4 * NB), :] = cols[
                pl.ds(bl * 256, 256), pl.ds(q * 128, 128)
            ]


def row_index(shape, dim):
    m = lax.broadcasted_iota(jnp.int32, shape, dim)
    bl = m // 4 % NB
    group, tl, q = m // (16 * NB), m // (4 * NB) % 4, m % 4
    return group * 16 + q * 4 + tl, bl


def day_matrices(basis_day):
    n = 128 * NB
    wide = row_index((n, 128), 0)[0] == lax.broadcasted_iota(jnp.int32, (n, 128), 1)
    tall = row_index((128, n), 1)[0] == lax.broadcasted_iota(jnp.int32, (128, n), 0)
    same = row_index((n, n), 0)[1] == row_index((n, n), 1)[1]
    wide, tall = wide.astype(BF16), tall.astype(BF16)

    def pick(half, dim):
        rows = lax.dot_general(wide, half, (((1,), (dim,)), ((), ())), preferred_element_type=F32)
        both = jnp.dot(rows.astype(BF16), tall, preferred_element_type=F32)
        return jnp.where(same, both, 0.0).astype(BF16)

    halves = split(basis_day)
    return [pick(h, 1) for h in halves], [pick(h, 0) for h in halves]


def middle(r_ref, bx_ref, bd_ref, ed_ref, ex_ref, ey_ref, noise_ref, out_ref, work):
    bx = split(bx_ref[...])
    to_s, to_t = day_matrices(bd_ref[...])
    day, bl = row_index((128 * NB, 128), 0)
    chosen = day == lax.broadcasted_iota(jnp.int32, day.shape, 1)
    ed = jnp.sum(jnp.where(chosen, ed_ref[...], 0.0), 1, keepdims=True)
    edx = ed * ex_ref[...]
    w = 4 * NB
    column = lax.broadcasted_iota(jnp.int32, ey_ref.shape, 1)
    mine = lax.axis_index(ORDER)

    def blocks(half):
        for zh, zl, core, x in itertools.product(range(4), range(2), range(2), range(4)):
            device = ((zh * 2 + zl) * 2 + core) * 16 + x * 4
            ys = [pl.ds((device + y) * WIDE + half * w, w) for y in range(4)]
            tls = [pl.ds(((zh * 2 + core) * 4 + tl) * w, w) for tl in range(4)]
            yield ys, tls, pl.ds((zl * 4 + x) * 128, 128)

    for half in range(WIDE // w):
        for ys, tls, lanes in blocks(half):
            for rows, part in zip(tls, swap_groups([r_ref[y, :] for y in ys])):
                work[rows, lanes] = part
        ey = jnp.zeros_like(ed)
        for i in range(NB):
            own = jnp.where(column == half * ROWS + i * 256 + mine, ey_ref[...], 0.0)
            ey = jnp.where(bl[:, :1] == i, jnp.sum(own, 1, keepdims=True), ey)
        along_x = dot3(split(work[...]), bx)
        spectral = dot3(to_s, split(along_x))
        back_day = dot3(to_t, split(spectral / (edx * ey + noise_ref[:1, :1])))
        work[...] = dot3(split(back_day), bx, ((1,), (1,)))
        for ys, tls, lanes in blocks(half):
            for rows, part in zip(ys, swap_groups([work[t, lanes] for t in tls])):
                out_ref[rows, :] = part


def inverse_y(r_ref, by_ref, out_ref, cols, high, low):
    @pl.when(pl.program_id(0) == 0)
    def _():
        for bl in range(WIDE // 4):
            for q in range(4):
                cols[pl.ds(bl * 256, 256), pl.ds(q * 128, 128)] = r_ref[
                    pl.ds(bl * 4 + q, 256, stride=WIDE), :
                ]
        high[...], low[...] = split(cols[...].T)

    out_ref[...] = dot3((high[...], low[...]), split(by_ref[...]), ((1,), (1,)))


VMEM = pl.BlockSpec(memory_space=pltpu.VMEM)


def limit(mib):
    return pltpu.CompilerParams(vmem_limit_bytes=mib << 20)


def exchange(parts):
    parts = parts.reshape(256, WIDE, 128)
    return lax.all_to_all(parts, ORDER, 0, 0, tiled=True).reshape(256 * WIDE, 128)


def body(field, basis_day, basis_x, basis_y, eig_day, eig_x, eig_y, noise):
    days, rows, cols = field.shape
    flat = field.reshape(days * rows, cols)
    sent, level = pl.pallas_call(
        forward_y,
        out_shape=[jax.ShapeDtypeStruct((256, WIDE, 128), F32), jax.ShapeDtypeStruct((8, 128), F32)],
        grid=(cols // ROWS,),
        in_specs=[
            pl.BlockSpec(memory_space=pltpu.SMEM),
            pl.BlockSpec(flat.shape, lambda c: (0, 0)),
            pl.BlockSpec((cols, ROWS), lambda c: (0, c)),
        ],
        out_specs=[
            pl.BlockSpec((256, 4 * NB, 128), lambda c: (0, c, 0)),
            pl.BlockSpec((8, 128), lambda c: (0, 0)),
        ],
        scratch_shapes=[pltpu.VMEM((ROWS, days * rows), F32)],
        compiler_params=limit(60),
        name="forward_y",
    )(noise, flat, basis_y)
    solved = pl.pallas_call(
        middle,
        out_shape=jax.ShapeDtypeStruct((256 * WIDE, 128), F32),
        in_specs=[VMEM] * 7,
        out_specs=VMEM,
        scratch_shapes=[pltpu.VMEM((128 * NB, cols), F32)],
        compiler_params=limit(32),
        name="middle",
    )(
        exchange(sent),
        basis_x,
        basis_day,
        eig_day.reshape(1, -1),
        eig_x.reshape(1, -1),
        eig_y.reshape(1, -1),
        level,
    )
    weights = pl.pallas_call(
        inverse_y,
        out_shape=jax.ShapeDtypeStruct(flat.shape, F32),
        grid=(2,),
        in_specs=[
            pl.BlockSpec((256 * WIDE, 128), lambda c: (0, 0)),
            pl.BlockSpec((cols // 2, cols), lambda c: (c, 0)),
        ],
        out_specs=pl.BlockSpec((days * rows, cols // 2), lambda c: (0, c)),
        scratch_shapes=[
            pltpu.VMEM((cols, days * rows), F32),
            pltpu.VMEM((days * rows, cols), BF16),
            pltpu.VMEM((days * rows, cols), BF16),
        ],
        compiler_params=limit(40),
        name="inverse_y",
    )(exchange(solved), basis_y)
    return weights.reshape(days, rows, cols)


def solution(mesh):
    fine = Mesh(mesh.devices.reshape(4, 2, 2, 4, 4), AXES)
    spec = P(("zh", "core"), ("zl", "x", "y"), None)
    in_specs = (spec, P(), P(), P(), P(), P(), P(), P())
    return jax.shard_map(body, mesh=fine, in_specs=in_specs, out_specs=spec, check_vma=False)
```

```python
import functools
import itertools

import jax
import jax.numpy as jnp
from jax import lax
from jax.experimental import pallas as pl
from jax.experimental.pallas import tpu as pltpu
from jax.sharding import Mesh, PartitionSpec as P

F32, BF16 = jnp.float32, jnp.bfloat16
AXES = ("zh", "core", "zl", "x", "y")
ORDER = ("zh", "zl", "core", "x", "y")
NB = 2
ROWS = NB * 256
WIDE = 16


def split(v):
    hi = v.astype(BF16)
    return hi, (v - hi.astype(F32)).astype(BF16)


def dot3(a, b, dims=((1,), (0,))):
    mul = functools.partial(
        lax.dot_general, dimension_numbers=(dims, ((), ())), preferred_element_type=F32
    )
    return mul(a[0], b[0]) + (mul(a[0], b[1]) + mul(a[1], b[0]))


def swap_groups(v):
    group = lax.broadcasted_iota(jnp.int32, v[0].shape, 1) // 32
    low, even = group < 2, group % 2 == 0

    def pair(a, b, keep, left, right):
        return (
            jnp.where(keep, a, pltpu.roll(b, right, 1)),
            jnp.where(keep, pltpu.roll(a, left, 1), b),
        )

    a0, a2 = pair(v[0], v[2], low, 64, 64)
    a1, a3 = pair(v[1], v[3], low, 64, 64)
    w0, w1 = pair(a0, a1, even, 96, 32)
    w2, w3 = pair(a2, a3, even, 96, 32)
    return w0, w1, w2, w3


def forward_y(_, f_ref, by_ref, out_ref, cols):
    cols[...] = dot3(split(by_ref[...]), split(f_ref[...]), ((0,), (1,)))
    out = out_ref.reshape(256 * 4 * NB, 128)
    for bl in range(NB):
        for q in range(4):
            out[pl.ds(bl * 4 + q, 256, stride=4 * NB), :] = cols[
                pl.ds(bl * 256, 256), pl.ds(q * 128, 128)
            ]


def row_index(shape, dim):
    m = lax.broadcasted_iota(jnp.int32, shape, dim)
    bl = m // 4 % NB
    group, tl, q = m // (16 * NB), m // (4 * NB) % 4, m % 4
    return group * 16 + q * 4 + tl, bl


def day_matrices(basis_day):
    n = 128 * NB
    wide = row_index((n, 128), 0)[0] == lax.broadcasted_iota(jnp.int32, (n, 128), 1)
    tall = row_index((128, n), 1)[0] == lax.broadcasted_iota(jnp.int32, (128, n), 0)
    same = row_index((n, n), 0)[1] == row_index((n, n), 1)[1]
    wide, tall = wide.astype(BF16), tall.astype(BF16)

    def pick(half, dim):
        rows = lax.dot_general(wide, half, (((1,), (dim,)), ((), ())), preferred_element_type=F32)
        both = jnp.dot(rows.astype(BF16), tall, preferred_element_type=F32)
        return jnp.where(same, both, 0.0).astype(BF16)

    halves = split(basis_day)
    return [pick(h, 1) for h in halves], [pick(h, 0) for h in halves]


def middle(r_ref, bx_ref, bd_ref, ed_ref, ex_ref, ey_ref, noise_ref, out_ref, work):
    bx = split(bx_ref[...])
    to_s, to_t = day_matrices(bd_ref[...])
    day, bl = row_index((128 * NB, 128), 0)
    chosen = day == lax.broadcasted_iota(jnp.int32, day.shape, 1)
    ed = jnp.sum(jnp.where(chosen, ed_ref[...], 0.0), 1, keepdims=True)
    edx = ed * ex_ref[...]
    w = 4 * NB
    column = lax.broadcasted_iota(jnp.int32, ey_ref.shape, 1)
    mine = lax.axis_index(ORDER)

    def blocks(half):
        for zh, zl, core, x in itertools.product(range(4), range(2), range(2), range(4)):
            device = ((zh * 2 + zl) * 2 + core) * 16 + x * 4
            ys = [pl.ds((device + y) * WIDE + half * w, w) for y in range(4)]
            tls = [pl.ds(((zh * 2 + core) * 4 + tl) * w, w) for tl in range(4)]
            yield ys, tls, pl.ds((zl * 4 + x) * 128, 128)

    for half in range(WIDE // w):
        for ys, tls, lanes in blocks(half):
            for rows, part in zip(tls, swap_groups([r_ref[y, :] for y in ys])):
                work[rows, lanes] = part
        ey = jnp.zeros_like(ed)
        for i in range(NB):
            own = jnp.where(column == half * ROWS + i * 256 + mine, ey_ref[...], 0.0)
            ey = jnp.where(bl[:, :1] == i, jnp.sum(own, 1, keepdims=True), ey)
        along_x = dot3(split(work[...]), bx)
        spectral = dot3(to_s, split(along_x))
        back_day = dot3(to_t, split(spectral / (edx * ey + noise_ref[0])))
        work[...] = dot3(split(back_day), bx, ((1,), (1,)))
        for ys, tls, lanes in blocks(half):
            for rows, part in zip(ys, swap_groups([work[t, lanes] for t in tls])):
                out_ref[rows, :] = part


def inverse_y(r_ref, by_ref, out_ref, cols, high, low):
    @pl.when(pl.program_id(0) == 0)
    def _():
        for bl in range(WIDE // 4):
            for q in range(4):
                cols[pl.ds(bl * 256, 256), pl.ds(q * 128, 128)] = r_ref[
                    pl.ds(bl * 4 + q, 256, stride=WIDE), :
                ]
        high[...], low[...] = split(cols[...].T)

    out_ref[...] = dot3((high[...], low[...]), split(by_ref[...]), ((1,), (1,)))


VMEM = pl.BlockSpec(memory_space=pltpu.VMEM)


def limit(mib):
    return pltpu.CompilerParams(vmem_limit_bytes=mib << 20)


def exchange(parts):
    parts = parts.reshape(256, WIDE, 128)
    return lax.all_to_all(parts, ORDER, 0, 0, tiled=True).reshape(256 * WIDE, 128)


def body(field, basis_day, basis_x, basis_y, eig_day, eig_x, eig_y, noise):
    days, rows, cols = field.shape
    flat = field.reshape(days * rows, cols)
    sent = pl.pallas_call(
        forward_y,
        out_shape=jax.ShapeDtypeStruct((256, WIDE, 128), F32),
        grid=(cols // ROWS,),
        in_specs=[
            pl.BlockSpec(memory_space=pltpu.SMEM),
            pl.BlockSpec(flat.shape, lambda c: (0, 0)),
            pl.BlockSpec((cols, ROWS), lambda c: (0, c)),
        ],
        out_specs=pl.BlockSpec((256, 4 * NB, 128), lambda c: (0, c, 0)),
        scratch_shapes=[pltpu.VMEM((ROWS, days * rows), F32)],
        compiler_params=limit(60),
        name="forward_y",
    )(noise, flat, basis_y)
    solved = pl.pallas_call(
        middle,
        out_shape=jax.ShapeDtypeStruct((256 * WIDE, 128), F32),
        in_specs=[VMEM] * 6 + [pl.BlockSpec(memory_space=pltpu.SMEM)],
        out_specs=VMEM,
        scratch_shapes=[pltpu.VMEM((128 * NB, cols), F32)],
        compiler_params=limit(32),
        name="middle",
    )(
        exchange(sent),
        basis_x,
        basis_day,
        eig_day.reshape(1, -1),
        eig_x.reshape(1, -1),
        eig_y.reshape(1, -1),
        noise,
    )
    weights = pl.pallas_call(
        inverse_y,
        out_shape=jax.ShapeDtypeStruct(flat.shape, F32),
        grid=(2,),
        in_specs=[
            pl.BlockSpec((256 * WIDE, 128), lambda c: (0, 0)),
            pl.BlockSpec((cols // 2, cols), lambda c: (c, 0)),
        ],
        out_specs=pl.BlockSpec((days * rows, cols // 2), lambda c: (0, c)),
        scratch_shapes=[
            pltpu.VMEM((cols, days * rows), F32),
            pltpu.VMEM((days * rows, cols), BF16),
            pltpu.VMEM((days * rows, cols), BF16),
        ],
        compiler_params=limit(40),
        name="inverse_y",
    )(exchange(solved), basis_y)
    return weights.reshape(days, rows, cols)


def solution(mesh):
    fine = Mesh(mesh.devices.reshape(4, 2, 2, 4, 4), AXES)
    spec = P(("zh", "core"), ("zl", "x", "y"), None)
    in_specs = (spec, P(), P(), P(), P(), P(), P(), P())
    return jax.shard_map(body, mesh=fine, in_specs=in_specs, out_specs=spec, check_vma=False)
```

```python
import functools
import itertools

import jax
import jax.numpy as jnp
from jax import lax
from jax.experimental import pallas as pl
from jax.experimental.pallas import tpu as pltpu
from jax.sharding import Mesh, PartitionSpec as P

F32, BF16 = jnp.float32, jnp.bfloat16
AXES = ("zh", "core", "zl", "x", "y")
ORDER = ("zh", "zl", "core", "x", "y")
NB = 2
ROWS = NB * 256
PIECES = 2
WIDE = 16


def split(v):
    hi = v.astype(BF16)
    return hi, (v - hi.astype(F32)).astype(BF16)


def dot3(a, b, dims=((1,), (0,))):
    mul = functools.partial(
        lax.dot_general, dimension_numbers=(dims, ((), ())), preferred_element_type=F32
    )
    return mul(a[0], b[0]) + (mul(a[0], b[1]) + mul(a[1], b[0]))


def swap_groups(v):
    group = lax.broadcasted_iota(jnp.int32, v[0].shape, 1) // 32
    low, even = group < 2, group % 2 == 0

    def pair(a, b, keep, left, right):
        return (
            jnp.where(keep, a, pltpu.roll(b, right, 1)),
            jnp.where(keep, pltpu.roll(a, left, 1), b),
        )

    a0, a2 = pair(v[0], v[2], low, 64, 64)
    a1, a3 = pair(v[1], v[3], low, 64, 64)
    w0, w1 = pair(a0, a1, even, 96, 32)
    w2, w3 = pair(a2, a3, even, 96, 32)
    return w0, w1, w2, w3


def forward_y(_, f_hbm, by_hbm, out_ref, field, by, high, low, sems):
    step = f_hbm.shape[1] // PIECES
    pieces = [pl.ds(i * step, step) for i in range(PIECES)]

    def load_field(i):
        return pltpu.make_async_copy(f_hbm.at[:, pieces[i]], field.at[:, pieces[i]], sems.at[0, i])

    def load_by(half, i):
        return pltpu.make_async_copy(
            by_hbm.at[pieces[i], pl.ds(half * ROWS, ROWS)], by.at[half, pieces[i], :], sems.at[1 + half, i]
        )

    def work(half):
        cols = None
        for i, piece in enumerate(pieces):
            if half == 0:
                load_field(i).wait()
                high[:, piece], low[:, piece] = split(field[:, piece])
            load_by(half, i).wait()
            part = dot3(split(by[half, piece, :]), (high[:, piece], low[:, piece]), ((0,), (1,)))
            cols = part if cols is None else cols + part
        out = out_ref.reshape(256 * 4 * NB, 128)
        for bl in range(NB):
            for q in range(4):
                out[pl.ds(bl * 4 + q, 256, stride=4 * NB), :] = cols[
                    bl * 256 : (bl + 1) * 256, q * 128 : (q + 1) * 128
                ]

    @pl.when(pl.program_id(0) == 0)
    def _():
        for i in range(PIECES):
            load_field(i).start()
            load_by(0, i).start()
        for i in range(PIECES):
            load_by(1, i).start()
        work(0)

    @pl.when(pl.program_id(0) == 1)
    def _():
        work(1)


def row_index(shape, dim):
    m = lax.broadcasted_iota(jnp.int32, shape, dim)
    bl = m // 4 % NB
    group, tl, q = m // (16 * NB), m // (4 * NB) % 4, m % 4
    return group * 16 + q * 4 + tl, bl


def day_matrices(basis_day):
    n = 128 * NB
    wide = row_index((n, 128), 0)[0] == lax.broadcasted_iota(jnp.int32, (n, 128), 1)
    tall = row_index((128, n), 1)[0] == lax.broadcasted_iota(jnp.int32, (128, n), 0)
    same = row_index((n, n), 0)[1] == row_index((n, n), 1)[1]
    wide, tall = wide.astype(BF16), tall.astype(BF16)

    def pick(half, dim):
        rows = lax.dot_general(wide, half, (((1,), (dim,)), ((), ())), preferred_element_type=F32)
        both = jnp.dot(rows.astype(BF16), tall, preferred_element_type=F32)
        return jnp.where(same, both, 0.0).astype(BF16)

    halves = split(basis_day)
    return [pick(h, 1) for h in halves], [pick(h, 0) for h in halves]


def middle(r_ref, bx_ref, bd_ref, ed_ref, ex_ref, ey_ref, noise_ref, out_ref, work):
    bx = split(bx_ref[...])
    to_s, to_t = day_matrices(bd_ref[...])
    day, bl = row_index((128 * NB, 128), 0)
    chosen = day == lax.broadcasted_iota(jnp.int32, day.shape, 1)
    ed = jnp.sum(jnp.where(chosen, ed_ref[...], 0.0), 1, keepdims=True)
    edx = ed * ex_ref[...]
    w = 4 * NB
    column = lax.broadcasted_iota(jnp.int32, ey_ref.shape, 1)
    mine = lax.axis_index(ORDER)

    def blocks(half):
        for zh, zl, core, x in itertools.product(range(4), range(2), range(2), range(4)):
            device = ((zh * 2 + zl) * 2 + core) * 16 + x * 4
            ys = [pl.ds((device + y) * WIDE + half * w, w) for y in range(4)]
            tls = [pl.ds(((zh * 2 + core) * 4 + tl) * w, w) for tl in range(4)]
            yield ys, tls, pl.ds((zl * 4 + x) * 128, 128)

    for half in range(WIDE // w):
        for ys, tls, lanes in blocks(half):
            for rows, part in zip(tls, swap_groups([r_ref[y, :] for y in ys])):
                work[rows, lanes] = part
        ey = jnp.zeros_like(ed)
        for i in range(NB):
            own = jnp.where(column == half * ROWS + i * 256 + mine, ey_ref[...], 0.0)
            ey = jnp.where(bl[:, :1] == i, jnp.sum(own, 1, keepdims=True), ey)
        along_x = dot3(split(work[...]), bx)
        spectral = dot3(to_s, split(along_x))
        back_day = dot3(to_t, split(spectral / (edx * ey + noise_ref[0])))
        work[...] = dot3(split(back_day), bx, ((1,), (1,)))
        for ys, tls, lanes in blocks(half):
            for rows, part in zip(ys, swap_groups([work[t, lanes] for t in tls])):
                out_ref[rows, :] = part


def inverse_y(r_ref, by_ref, out_ref, cols, high, low):
    @pl.when(pl.program_id(0) == 0)
    def _():
        for bl in range(WIDE // 4):
            for q in range(4):
                cols[pl.ds(bl * 256, 256), pl.ds(q * 128, 128)] = r_ref[
                    pl.ds(bl * 4 + q, 256, stride=WIDE), :
                ]
        high[...], low[...] = split(cols[...].T)

    out_ref[...] = dot3((high[...], low[...]), split(by_ref[...]), ((1,), (1,)))


VMEM = pl.BlockSpec(memory_space=pltpu.VMEM)


def limit(mib):
    return pltpu.CompilerParams(vmem_limit_bytes=mib << 20)


def exchange(parts):
    parts = parts.reshape(256, WIDE, 128)
    return lax.all_to_all(parts, ORDER, 0, 0, tiled=True).reshape(256 * WIDE, 128)


def body(field, basis_day, basis_x, basis_y, eig_day, eig_x, eig_y, noise):
    days, rows, cols = field.shape
    flat = field.reshape(days * rows, cols)
    sent = pl.pallas_call(
        forward_y,
        out_shape=jax.ShapeDtypeStruct((256, WIDE, 128), F32),
        grid=(cols // ROWS,),
        in_specs=[
            pl.BlockSpec(memory_space=pltpu.SMEM),
            pl.BlockSpec(memory_space=pl.ANY),
            pl.BlockSpec(memory_space=pl.ANY),
        ],
        out_specs=pl.BlockSpec((256, 4 * NB, 128), lambda c: (0, c, 0)),
        scratch_shapes=[
            pltpu.VMEM(flat.shape, F32),
            pltpu.VMEM((2, cols, ROWS), F32),
            pltpu.VMEM(flat.shape, BF16),
            pltpu.VMEM(flat.shape, BF16),
            pltpu.SemaphoreType.DMA((3, PIECES)),
        ],
        compiler_params=limit(60),
        name="forward_y",
    )(noise, flat, basis_y)
    solved = pl.pallas_call(
        middle,
        out_shape=jax.ShapeDtypeStruct((256 * WIDE, 128), F32),
        in_specs=[VMEM] * 6 + [pl.BlockSpec(memory_space=pltpu.SMEM)],
        out_specs=VMEM,
        scratch_shapes=[pltpu.VMEM((128 * NB, cols), F32)],
        compiler_params=limit(32),
        name="middle",
    )(
        exchange(sent),
        basis_x,
        basis_day,
        eig_day.reshape(1, -1),
        eig_x.reshape(1, -1),
        eig_y.reshape(1, -1),
        noise,
    )
    weights = pl.pallas_call(
        inverse_y,
        out_shape=jax.ShapeDtypeStruct(flat.shape, F32),
        grid=(2,),
        in_specs=[
            pl.BlockSpec((256 * WIDE, 128), lambda c: (0, 0)),
            pl.BlockSpec((cols // 2, cols), lambda c: (c, 0)),
        ],
        out_specs=pl.BlockSpec((days * rows, cols // 2), lambda c: (0, c)),
        scratch_shapes=[
            pltpu.VMEM((cols, days * rows), F32),
            pltpu.VMEM((days * rows, cols), BF16),
            pltpu.VMEM((days * rows, cols), BF16),
        ],
        compiler_params=limit(40),
        name="inverse_y",
    )(exchange(solved), basis_y)
    return weights.reshape(days, rows, cols)


def solution(mesh):
    fine = Mesh(mesh.devices.reshape(4, 2, 2, 4, 4), AXES)
    spec = P(("zh", "core"), ("zl", "x", "y"), None)
    in_specs = (spec, P(), P(), P(), P(), P(), P(), P())
    return jax.shard_map(body, mesh=fine, in_specs=in_specs, out_specs=spec, check_vma=False)
```

```python
import functools
import itertools

import jax
import jax.numpy as jnp
from jax import lax
from jax.experimental import pallas as pl
from jax.experimental.pallas import tpu as pltpu
from jax.sharding import Mesh, PartitionSpec as P

F32, BF16 = jnp.float32, jnp.bfloat16
AXES = ("zh", "core", "zl", "x", "y")
ORDER = ("zh", "zl", "core", "x", "y")
NB = 2
ROWS = NB * 256
PIECES = 2
WIDE = 16


def split(v):
    hi = v.astype(BF16)
    return hi, (v - hi.astype(F32)).astype(BF16)


def dot3(a, b, dims=((1,), (0,))):
    mul = functools.partial(
        lax.dot_general, dimension_numbers=(dims, ((), ())), preferred_element_type=F32
    )
    return mul(a[0], b[0]) + (mul(a[0], b[1]) + mul(a[1], b[0]))


def dot3_long(a, b, dims=((1,), (0,))):
    left = jnp.concatenate([a[0], a[0], a[1]], dims[0][0])
    right = jnp.concatenate([b[0], b[1], b[0]], dims[1][0])
    return lax.dot_general(left, right, (dims, ((), ())), preferred_element_type=F32)


def swap_groups(v):
    group = lax.broadcasted_iota(jnp.int32, v[0].shape, 1) // 32
    low, even = group < 2, group % 2 == 0

    def pair(a, b, keep, left, right):
        return (
            jnp.where(keep, a, pltpu.roll(b, right, 1)),
            jnp.where(keep, pltpu.roll(a, left, 1), b),
        )

    a0, a2 = pair(v[0], v[2], low, 64, 64)
    a1, a3 = pair(v[1], v[3], low, 64, 64)
    w0, w1 = pair(a0, a1, even, 96, 32)
    w2, w3 = pair(a2, a3, even, 96, 32)
    return w0, w1, w2, w3


def forward_y(_, f_hbm, by_hbm, out_ref, field, by, high, low, sems):
    step = f_hbm.shape[1] // PIECES
    pieces = [pl.ds(i * step, step) for i in range(PIECES)]

    def load_field(i):
        return pltpu.make_async_copy(f_hbm.at[:, pieces[i]], field.at[:, pieces[i]], sems.at[0, i])

    def load_by(half, i):
        return pltpu.make_async_copy(
            by_hbm.at[pieces[i], pl.ds(half * ROWS, ROWS)], by.at[half, pieces[i], :], sems.at[1 + half, i]
        )

    def work(half):
        cols = None
        for i, piece in enumerate(pieces):
            if half == 0:
                load_field(i).wait()
                high[:, piece], low[:, piece] = split(field[:, piece])
            load_by(half, i).wait()
            part = dot3(split(by[half, piece, :]), (high[:, piece], low[:, piece]), ((0,), (1,)))
            cols = part if cols is None else cols + part
        out = out_ref.reshape(256 * 4 * NB, 128)
        for bl in range(NB):
            for q in range(4):
                out[pl.ds(bl * 4 + q, 256, stride=4 * NB), :] = cols[
                    bl * 256 : (bl + 1) * 256, q * 128 : (q + 1) * 128
                ]

    @pl.when(pl.program_id(0) == 0)
    def _():
        for i in range(PIECES):
            load_field(i).start()
            load_by(0, i).start()
        for i in range(PIECES):
            load_by(1, i).start()
        work(0)

    @pl.when(pl.program_id(0) == 1)
    def _():
        work(1)


def row_index(shape, dim):
    m = lax.broadcasted_iota(jnp.int32, shape, dim)
    bl = m // 4 % NB
    group, tl, q = m // (16 * NB), m // (4 * NB) % 4, m % 4
    return group * 16 + q * 4 + tl, bl


def day_matrices(basis_day):
    n = 128 * NB
    wide = row_index((n, 128), 0)[0] == lax.broadcasted_iota(jnp.int32, (n, 128), 1)
    tall = row_index((128, n), 1)[0] == lax.broadcasted_iota(jnp.int32, (128, n), 0)
    same = row_index((n, n), 0)[1] == row_index((n, n), 1)[1]
    wide, tall = wide.astype(BF16), tall.astype(BF16)

    def pick(half, dim):
        rows = lax.dot_general(wide, half, (((1,), (dim,)), ((), ())), preferred_element_type=F32)
        both = jnp.dot(rows.astype(BF16), tall, preferred_element_type=F32)
        return jnp.where(same, both, 0.0).astype(BF16)

    halves = split(basis_day)
    return [pick(h, 1) for h in halves], [pick(h, 0) for h in halves]


def middle(r_ref, bx_ref, bd_ref, ed_ref, ex_ref, ey_ref, noise_ref, out_ref, work):
    bx = split(bx_ref[...])
    to_s, to_t = day_matrices(bd_ref[...])
    day, bl = row_index((128 * NB, 128), 0)
    chosen = day == lax.broadcasted_iota(jnp.int32, day.shape, 1)
    ed = jnp.sum(jnp.where(chosen, ed_ref[...], 0.0), 1, keepdims=True)
    edx = ed * ex_ref[...]
    w = 4 * NB
    column = lax.broadcasted_iota(jnp.int32, ey_ref.shape, 1)
    mine = lax.axis_index(ORDER)

    def blocks(half):
        for zh, zl, core, x in itertools.product(range(4), range(2), range(2), range(4)):
            device = ((zh * 2 + zl) * 2 + core) * 16 + x * 4
            ys = [pl.ds((device + y) * WIDE + half * w, w) for y in range(4)]
            tls = [pl.ds(((zh * 2 + core) * 4 + tl) * w, w) for tl in range(4)]
            yield ys, tls, pl.ds((zl * 4 + x) * 128, 128)

    for half in range(WIDE // w):
        for ys, tls, lanes in blocks(half):
            for rows, part in zip(tls, swap_groups([r_ref[y, :] for y in ys])):
                work[rows, lanes] = part
        ey = jnp.zeros_like(ed)
        for i in range(NB):
            own = jnp.where(column == half * ROWS + i * 256 + mine, ey_ref[...], 0.0)
            ey = jnp.where(bl[:, :1] == i, jnp.sum(own, 1, keepdims=True), ey)
        along_x = dot3_long(split(work[...]), bx)
        spectral = dot3_long(to_s, split(along_x))
        back_day = dot3_long(to_t, split(spectral / (edx * ey + noise_ref[0])))
        work[...] = dot3_long(split(back_day), bx, ((1,), (1,)))
        for ys, tls, lanes in blocks(half):
            for rows, part in zip(ys, swap_groups([work[t, lanes] for t in tls])):
                out_ref[rows, :] = part


def inverse_y(r_ref, by_ref, out_ref, cols, high, low):
    @pl.when(pl.program_id(0) == 0)
    def _():
        for bl in range(WIDE // 4):
            for q in range(4):
                cols[pl.ds(bl * 256, 256), pl.ds(q * 128, 128)] = r_ref[
                    pl.ds(bl * 4 + q, 256, stride=WIDE), :
                ]
        high[...], low[...] = split(cols[...].T)

    out_ref[...] = dot3((high[...], low[...]), split(by_ref[...]), ((1,), (1,)))


VMEM = pl.BlockSpec(memory_space=pltpu.VMEM)


def limit(mib):
    return pltpu.CompilerParams(vmem_limit_bytes=mib << 20)


def exchange(parts):
    parts = parts.reshape(256, WIDE, 128)
    return lax.all_to_all(parts, ORDER, 0, 0, tiled=True).reshape(256 * WIDE, 128)


def body(field, basis_day, basis_x, basis_y, eig_day, eig_x, eig_y, noise):
    days, rows, cols = field.shape
    flat = field.reshape(days * rows, cols)
    sent = pl.pallas_call(
        forward_y,
        out_shape=jax.ShapeDtypeStruct((256, WIDE, 128), F32),
        grid=(cols // ROWS,),
        in_specs=[
            pl.BlockSpec(memory_space=pltpu.SMEM),
            pl.BlockSpec(memory_space=pl.ANY),
            pl.BlockSpec(memory_space=pl.ANY),
        ],
        out_specs=pl.BlockSpec((256, 4 * NB, 128), lambda c: (0, c, 0)),
        scratch_shapes=[
            pltpu.VMEM(flat.shape, F32),
            pltpu.VMEM((2, cols, ROWS), F32),
            pltpu.VMEM(flat.shape, BF16),
            pltpu.VMEM(flat.shape, BF16),
            pltpu.SemaphoreType.DMA((3, PIECES)),
        ],
        compiler_params=limit(60),
        name="forward_y",
    )(noise, flat, basis_y)
    solved = pl.pallas_call(
        middle,
        out_shape=jax.ShapeDtypeStruct((256 * WIDE, 128), F32),
        in_specs=[VMEM] * 6 + [pl.BlockSpec(memory_space=pltpu.SMEM)],
        out_specs=VMEM,
        scratch_shapes=[pltpu.VMEM((128 * NB, cols), F32)],
        compiler_params=limit(32),
        name="middle",
    )(
        exchange(sent),
        basis_x,
        basis_day,
        eig_day.reshape(1, -1),
        eig_x.reshape(1, -1),
        eig_y.reshape(1, -1),
        noise,
    )
    weights = pl.pallas_call(
        inverse_y,
        out_shape=jax.ShapeDtypeStruct(flat.shape, F32),
        grid=(2,),
        in_specs=[
            pl.BlockSpec((256 * WIDE, 128), lambda c: (0, 0)),
            pl.BlockSpec((cols // 2, cols), lambda c: (c, 0)),
        ],
        out_specs=pl.BlockSpec((days * rows, cols // 2), lambda c: (0, c)),
        scratch_shapes=[
            pltpu.VMEM((cols, days * rows), F32),
            pltpu.VMEM((days * rows, cols), BF16),
            pltpu.VMEM((days * rows, cols), BF16),
        ],
        compiler_params=limit(40),
        name="inverse_y",
    )(exchange(solved), basis_y)
    return weights.reshape(days, rows, cols)


def solution(mesh):
    fine = Mesh(mesh.devices.reshape(4, 2, 2, 4, 4), AXES)
    spec = P(("zh", "core"), ("zl", "x", "y"), None)
    in_specs = (spec, P(), P(), P(), P(), P(), P(), P())
    return jax.shard_map(body, mesh=fine, in_specs=in_specs, out_specs=spec, check_vma=False)
```

```python
import functools
import itertools

import jax
import jax.numpy as jnp
from jax import lax
from jax.experimental import pallas as pl
from jax.experimental.pallas import tpu as pltpu
from jax.sharding import Mesh, PartitionSpec as P

F32, BF16 = jnp.float32, jnp.bfloat16
AXES = ("zh", "core", "zl", "x", "y")
ORDER = ("zh", "zl", "core", "x", "y")
NB = 2
ROWS = NB * 256
PIECES = 2
WIDE = 16


def split(v):
    hi = v.astype(BF16)
    return hi, (v - hi.astype(F32)).astype(BF16)


def dot3(a, b, dims=((1,), (0,))):
    mul = functools.partial(
        lax.dot_general, dimension_numbers=(dims, ((), ())), preferred_element_type=F32
    )
    return mul(a[0], b[0]) + (mul(a[0], b[1]) + mul(a[1], b[0]))


def dot3_long(a, b, dims=((1,), (0,))):
    left = jnp.concatenate([a[0], a[0], a[1]], dims[0][0])
    right = jnp.concatenate([b[0], b[1], b[0]], dims[1][0])
    return lax.dot_general(left, right, (dims, ((), ())), preferred_element_type=F32)


def swap_groups(v):
    group = lax.broadcasted_iota(jnp.int32, v[0].shape, 1) // 32
    low, even = group < 2, group % 2 == 0

    def pair(a, b, keep, left, right):
        return (
            jnp.where(keep, a, pltpu.roll(b, right, 1)),
            jnp.where(keep, pltpu.roll(a, left, 1), b),
        )

    a0, a2 = pair(v[0], v[2], low, 64, 64)
    a1, a3 = pair(v[1], v[3], low, 64, 64)
    w0, w1 = pair(a0, a1, even, 96, 32)
    w2, w3 = pair(a2, a3, even, 96, 32)
    return w0, w1, w2, w3


def forward_y(_, f_hbm, by_hbm, out_ref, field, by, high, low, sems):
    step = f_hbm.shape[1] // PIECES
    pieces = [pl.ds(i * step, step) for i in range(PIECES)]

    def load_field(i):
        return pltpu.make_async_copy(f_hbm.at[:, pieces[i]], field.at[:, pieces[i]], sems.at[0, i])

    def load_by(half, i):
        return pltpu.make_async_copy(
            by_hbm.at[pieces[i], pl.ds(half * ROWS, ROWS)], by.at[half, pieces[i], :], sems.at[1 + half, i]
        )

    def work(half):
        cols = None
        for i, piece in enumerate(pieces):
            if half == 0:
                load_field(i).wait()
                high[:, piece], low[:, piece] = split(field[:, piece])
            load_by(half, i).wait()
            part = dot3(split(by[half, piece, :]), (high[:, piece], low[:, piece]), ((0,), (1,)))
            cols = part if cols is None else cols + part
        out = out_ref.reshape(256 * 4 * NB, 128)
        for bl in range(NB):
            for q in range(4):
                out[pl.ds(bl * 4 + q, 256, stride=4 * NB), :] = cols[
                    bl * 256 : (bl + 1) * 256, q * 128 : (q + 1) * 128
                ]

    @pl.when(pl.program_id(0) == 0)
    def _():
        for i in range(PIECES):
            load_field(i).start()
            load_by(0, i).start()
        for i in range(PIECES):
            load_by(1, i).start()
        work(0)

    @pl.when(pl.program_id(0) == 1)
    def _():
        work(1)


def row_index(shape, dim):
    m = lax.broadcasted_iota(jnp.int32, shape, dim)
    bl = m // 4 % NB
    group, tl, q = m // (16 * NB), m // (4 * NB) % 4, m % 4
    return group * 16 + q * 4 + tl, bl


def day_matrices(basis_day):
    n = 128 * NB
    wide = row_index((n, 128), 0)[0] == lax.broadcasted_iota(jnp.int32, (n, 128), 1)
    tall = row_index((128, n), 1)[0] == lax.broadcasted_iota(jnp.int32, (128, n), 0)
    same = row_index((n, n), 0)[1] == row_index((n, n), 1)[1]
    wide, tall = wide.astype(BF16), tall.astype(BF16)

    def pick(half, dim):
        rows = lax.dot_general(wide, half, (((1,), (dim,)), ((), ())), preferred_element_type=F32)
        both = jnp.dot(rows.astype(BF16), tall, preferred_element_type=F32)
        return jnp.where(same, both, 0.0).astype(BF16)

    halves = split(basis_day)
    return [pick(h, 1) for h in halves], [pick(h, 0) for h in halves]


def middle(r_ref, bx_ref, bd_ref, ed_ref, ex_ref, ey_ref, noise_ref, out_ref, work):
    bx = split(bx_ref[...])
    to_s, to_t = day_matrices(bd_ref[...])
    day, bl = row_index((128 * NB, 128), 0)
    chosen = day == lax.broadcasted_iota(jnp.int32, day.shape, 1)
    ed = jnp.sum(jnp.where(chosen, ed_ref[...], 0.0), 1, keepdims=True)
    edx = ed * ex_ref[...]
    w = 4 * NB
    column = lax.broadcasted_iota(jnp.int32, ey_ref.shape, 1)
    mine = lax.axis_index(ORDER)

    def blocks(half):
        for zh, zl, core, x in itertools.product(range(4), range(2), range(2), range(4)):
            device = ((zh * 2 + zl) * 2 + core) * 16 + x * 4
            ys = [pl.ds((device + y) * WIDE + half * w, w) for y in range(4)]
            tls = [pl.ds(((zh * 2 + core) * 4 + tl) * w, w) for tl in range(4)]
            yield ys, tls, pl.ds((zl * 4 + x) * 128, 128)

    for half in range(WIDE // w):
        for ys, tls, lanes in blocks(half):
            for rows, part in zip(tls, swap_groups([r_ref[y, :] for y in ys])):
                work[rows, lanes] = part
        ey = jnp.zeros_like(ed)
        for i in range(NB):
            own = jnp.where(column == half * ROWS + i * 256 + mine, ey_ref[...], 0.0)
            ey = jnp.where(bl[:, :1] == i, jnp.sum(own, 1, keepdims=True), ey)
        along_x = dot3_long(split(work[...]), bx)
        spectral = dot3_long(to_s, split(along_x))
        back_day = dot3_long(to_t, split(spectral / (edx * ey + noise_ref[0])))
        work[...] = dot3_long(split(back_day), bx, ((1,), (1,)))
        for ys, tls, lanes in blocks(half):
            for rows, part in zip(ys, swap_groups([work[t, lanes] for t in tls])):
                out_ref[rows, :] = part


def inverse_y(r_ref, by_ref, out_ref, cols, left):
    @pl.when(pl.program_id(0) == 0)
    def _():
        for bl in range(WIDE // 4):
            for q in range(4):
                cols[pl.ds(bl * 256, 256), pl.ds(q * 128, 128)] = r_ref[
                    pl.ds(bl * 4 + q, 256, stride=WIDE), :
                ]
        high, low = split(cols[...].T)
        n = high.shape[1]
        left[:, :n], left[:, n : 2 * n], left[:, 2 * n :] = high, high, low

    high, low = split(by_ref[...])
    right = jnp.concatenate([high, low, high], 1)
    out_ref[...] = lax.dot_general(left[...], right, (((1,), (1,)), ((), ())), preferred_element_type=F32)


VMEM = pl.BlockSpec(memory_space=pltpu.VMEM)


def limit(mib):
    return pltpu.CompilerParams(vmem_limit_bytes=mib << 20)


def exchange(parts):
    parts = parts.reshape(256, WIDE, 128)
    return lax.all_to_all(parts, ORDER, 0, 0, tiled=True).reshape(256 * WIDE, 128)


def body(field, basis_day, basis_x, basis_y, eig_day, eig_x, eig_y, noise):
    days, rows, cols = field.shape
    flat = field.reshape(days * rows, cols)
    sent = pl.pallas_call(
        forward_y,
        out_shape=jax.ShapeDtypeStruct((256, WIDE, 128), F32),
        grid=(cols // ROWS,),
        in_specs=[
            pl.BlockSpec(memory_space=pltpu.SMEM),
            pl.BlockSpec(memory_space=pl.ANY),
            pl.BlockSpec(memory_space=pl.ANY),
        ],
        out_specs=pl.BlockSpec((256, 4 * NB, 128), lambda c: (0, c, 0)),
        scratch_shapes=[
            pltpu.VMEM(flat.shape, F32),
            pltpu.VMEM((2, cols, ROWS), F32),
            pltpu.VMEM(flat.shape, BF16),
            pltpu.VMEM(flat.shape, BF16),
            pltpu.SemaphoreType.DMA((3, PIECES)),
        ],
        compiler_params=limit(60),
        name="forward_y",
    )(noise, flat, basis_y)
    solved = pl.pallas_call(
        middle,
        out_shape=jax.ShapeDtypeStruct((256 * WIDE, 128), F32),
        in_specs=[VMEM] * 6 + [pl.BlockSpec(memory_space=pltpu.SMEM)],
        out_specs=VMEM,
        scratch_shapes=[pltpu.VMEM((128 * NB, cols), F32)],
        compiler_params=limit(32),
        name="middle",
    )(
        exchange(sent),
        basis_x,
        basis_day,
        eig_day.reshape(1, -1),
        eig_x.reshape(1, -1),
        eig_y.reshape(1, -1),
        noise,
    )
    weights = pl.pallas_call(
        inverse_y,
        out_shape=jax.ShapeDtypeStruct(flat.shape, F32),
        grid=(2,),
        in_specs=[
            pl.BlockSpec((256 * WIDE, 128), lambda c: (0, 0)),
            pl.BlockSpec((cols // 2, cols), lambda c: (c, 0)),
        ],
        out_specs=pl.BlockSpec((days * rows, cols // 2), lambda c: (0, c)),
        scratch_shapes=[
            pltpu.VMEM((cols, days * rows), F32),
            pltpu.VMEM((days * rows, 3 * cols), BF16),
        ],
        compiler_params=limit(40),
        name="inverse_y",
    )(exchange(solved), basis_y)
    return weights.reshape(days, rows, cols)


def solution(mesh):
    fine = Mesh(mesh.devices.reshape(4, 2, 2, 4, 4), AXES)
    spec = P(("zh", "core"), ("zl", "x", "y"), None)
    in_specs = (spec, P(), P(), P(), P(), P(), P(), P())
    return jax.shard_map(body, mesh=fine, in_specs=in_specs, out_specs=spec, check_vma=False)
```
